128 devices in a mesh: row: 16 (over x, z_lo, core), col: 8 (over z_hi, y).
Axes of the slice: x: 4, y: 4, z: 4 (z_hi: 2, z_lo: 2; z = z_hi * 2 + z_lo), core: 2. Of those that a mesh axis runs over, the one named last changes fastest.
Arguments:
- precision: float32 [16384, 16384], P('row', 'col'), may hold values from -0.3 to 4, as said below
- samples: bfloat16 [1024, 16384], P(None, 'col'), may hold values from -6 to 6
- step_size: float32 [1], replicated, may hold values from 0.5 to 1
- threshold: float32 [1], replicated, may hold values from 0.1 to 0.3
Outputs:
- updated: float32 [16384, 16384], P('row', 'col')
The draws below stay inside these ranges and needn't reach their ends.
Inputs may be any that keep to these rules, and one draw needn't show every extreme that they name: precision is symmetric; its diagonal entries lie between 1 and 4.
All inputs are finite; a program needn't handle non-finite values.
Results may differ from the reference program's by a relative error of at most 0.0056.
Values may be sent and summed in bfloat16 or wider, within the bound.
No kernel may reach another device: no remote copies, remote signals or barrier semaphores. Data moves between devices by JAX's collectives and lax.ppermute only.
A program may use at most 192 MiB of HBM per device.

```python
import math
import jax
import jax.numpy as jnp
from jax import lax

P_SIZE = 16384
NSAMP = 1024
N_ROW = 16


def draw_precision(key, part):
    first_key = jax.random.fold_in(key, 11)
    second_key = jax.random.fold_in(key, 12)
    spread = jnp.clip(0.05 * jax.random.normal(first_key, (P_SIZE, P_SIZE), jnp.float32), -0.3, 0.3)
    spread = 0.5 * (spread + spread.T)
    diag_values = jnp.exp(jax.random.uniform(second_key, (P_SIZE,), jnp.float32, 0.0, math.log(4.0)))
    indices = jnp.arange(P_SIZE, dtype=jnp.int32)
    on_diagonal = indices[:, None] == indices[None, :]
    return jnp.where(on_diagonal, diag_values[:, None], spread)


def block_levels(key, extent, pieces, smallest, high):
    loudness, own = 1.0, jax.random.fold_in(key, 6)
    for dim, parts in pieces:
        heights = jnp.exp(jax.random.uniform(jax.random.fold_in(own, dim), (parts,), jnp.float32, smallest / len(pieces), high / len(pieces)))
        loudness = loudness * jnp.repeat(heights, extent[dim] // parts).reshape([-1 if axis == dim else 1 for axis in range(len(extent))])
    return loudness


def scatter_about(own_key, shape, width, most, pieces=(), held_as=jnp.bfloat16):
    entries = width * jax.random.normal(own_key, shape, jnp.float32)
    if pieces:
        entries = entries * block_levels(own_key, shape, pieces, -0.22, 0.18)
    return jnp.clip(entries, -most, most).astype(held_as)


def setup_inputs(seed: int = 0) -> dict:
    arg_keys = jax.random.split(jax.random.key(seed), 5)
    return {
        "precision": draw_precision(jax.random.fold_in(arg_keys[4], 71), 0),
        "samples": scatter_about(arg_keys[1], (NSAMP, P_SIZE), 1.0, 6.0, ((1, 8),)),
        "step_size": jnp.clip(jax.random.uniform(arg_keys[2], (1,), jnp.float32, 0.5, 1.0), 0.5, 1.0),
        "threshold": jnp.clip(jax.random.uniform(arg_keys[3], (1,), jnp.float32, 0.1, 0.3), 0.1, 0.3),
    }


def reference(precision, samples, step_size, threshold):
    sample_count = samples.shape[0]
    rounded = precision.astype(jnp.bfloat16)
    projected = lax.dot_general(samples, rounded, (((1,), (1,)), ((), ())), preferred_element_type=jnp.float32).astype(jnp.bfloat16)
    band_rows = P_SIZE // N_ROW
    all_cols = jnp.arange(P_SIZE, dtype=jnp.int32)

    def one_band(index):
        offset_row = (index * band_rows).astype(jnp.int32)
        proj_band = lax.dynamic_slice_in_dim(projected, offset_row, band_rows, 1)
        data_band = lax.dynamic_slice_in_dim(samples, offset_row, band_rows, 1)
        cross_rows = lax.dot_general(proj_band, samples, (((0,), (0,)), ((), ())), preferred_element_type=jnp.float32) / sample_count
        cross_cols = lax.dot_general(data_band, projected, (((0,), (0,)), ((), ())), preferred_element_type=jnp.float32) / sample_count
        symmetric = 0.5 * (cross_rows + cross_cols)
        current = lax.dynamic_slice_in_dim(precision, offset_row, band_rows, 0)
        global_row = offset_row + jnp.arange(band_rows, dtype=jnp.int32)
        on_diagonal = global_row[:, None] == all_cols[None, :]
        gradient = symmetric - jnp.where(on_diagonal, 1.0 / jnp.where(on_diagonal, current, 1.0), 0.0)
        stepped = current - step_size[0] * gradient
        shrunk = jnp.sign(stepped) * jnp.maximum(jnp.abs(stepped) - step_size[0] * threshold[0], 0.0)
        return jnp.where(on_diagonal, stepped, shrunk)

    bands = lax.map(one_band, jnp.arange(N_ROW, dtype=jnp.int32))
    return bands.reshape(P_SIZE, P_SIZE)
```

```python
import functools
import itertools

import jax
import jax.numpy as jnp
from jax import lax
from jax.experimental import pallas as pl
from jax.experimental.pallas import tpu as pltpu
from jax.sharding import Mesh
from jax.sharding import PartitionSpec as P


SIZES = (4, 2, 2, 2, 4)
NAMES = ("x", "zl", "core", "zh", "y")
ROW = ("x", "zl", "core")
COL = ("zh", "y")


def number(x, zl, h, zh, y):
    return (((x * 2 + zl) * 2 + h) * 2 + zh) * 4 + y


def places():
    return itertools.product(*(range(n) for n in SIZES))


def crossing_of_sums():
    return [
        (number(x, zl, h, zh, y), number(y, zh, h, x // 2, x % 2 * 2 + zl))
        for x, zl, h, zh, y in places()
    ]


def crossing_of_samples():
    return [
        (number(x, zl, h, zh, y), number(zh * 2 + y // 2, y % 2, h, zl, x))
        for x, zl, h, zh, y in places()
    ]


def sent_to_all(array, axes, length):
    copies = jnp.broadcast_to(array[None], (length, *array.shape))
    return lax.all_to_all(copies, axes, 0, 0, tiled=True)


TILE = 256


def update_kernel(samples_count, whole, scalars, yr, xr, xc, mine, other, precision, out):
    width = mine.shape[1]
    m, t = pl.program_id(0), pl.program_id(1)
    side = (whole[0] + t) % 2
    rows = pl.ds(pl.multiple_of(m * TILE, TILE), TILE)
    contract = (((0,), (0,)), ((), ()))

    def finish(panel):
        total = lax.dot_general(
            yr[:, rows],
            xc[:, pl.ds(pl.multiple_of(side * width, width), width)],
            contract,
            preferred_element_type=jnp.float32,
        )
        total = total + lax.dot_general(
            xr[:, rows], panel[...], contract, preferred_element_type=jnp.float32
        )
        gradient = total * (1.0 / samples_count)
        step, level = scalars[0], scalars[1]
        first_row = whole[1] + m * TILE
        first_col = whole[2] + side * width
        stepped = precision[...] - step * gradient
        out[...] = stepped - jnp.clip(stepped, -level, level)

        @pl.when((first_row < first_col + width) & (first_col < first_row + TILE))
        def _():
            row = first_row + lax.broadcasted_iota(jnp.int32, stepped.shape, 0)
            col = first_col + lax.broadcasted_iota(jnp.int32, stepped.shape, 1)
            own = precision[...]
            on_diagonal = row == col
            lowered = own - step * (gradient - 1.0 / jnp.where(on_diagonal, own, 1.0))
            out[...] = jnp.where(on_diagonal, lowered, out[...])

    @pl.when(t == 0)
    def _():
        finish(mine)

    @pl.when(t == 1)
    def _():
        finish(other)


def updated_tile(whole, scalars, yr, xr, xc, mine, other, precision):
    rows, cols = precision.shape
    width = mine.shape[1]
    inside = pl.BlockSpec(memory_space=pltpu.VMEM)
    tile = pl.BlockSpec((TILE, width), lambda m, t, whole: (m, (whole[0] + t) % 2))
    depth = 2 * xc.shape[0]
    return pl.pallas_call(
        functools.partial(update_kernel, xc.shape[0]),
        out_shape=jax.ShapeDtypeStruct(precision.shape, precision.dtype),
        grid_spec=pltpu.PrefetchScalarGridSpec(
            num_scalar_prefetch=1,
            grid=(rows // TILE, cols // width),
            in_specs=[pl.BlockSpec(memory_space=pltpu.SMEM)] + [inside] * 5 + [tile],
            out_specs=tile,
        ),
        compiler_params=pltpu.CompilerParams(vmem_limit_bytes=48 << 20),
        cost_estimate=pl.CostEstimate(
            flops=2 * rows * cols * depth, bytes_accessed=28 << 20, transcendentals=0
        ),
        name="update",
    )(whole, scalars, yr, xr, xc, mine, other, precision)


def per_device(precision, samples, step_size, threshold):
    rows_tile, cols_tile = precision.shape
    sample_count = samples.shape[0]
    x, zl, h, zh, y = (lax.axis_index(a) for a in NAMES)
    parts = 8
    piece = sample_count // parts

    mine = lax.dynamic_slice(
        samples, (x * 2 * piece, h * rows_tile), (2 * piece, rows_tile)
    )
    own_quarter = lax.ppermute(mine, NAMES, crossing_of_samples())
    rounded = precision.astype(jnp.bfloat16)
    partial = lax.dot_general(
        samples, rounded, (((1,), (1,)), ((), ())), preferred_element_type=jnp.float32
    ).astype(jnp.bfloat16)
    shares = lax.all_to_all(
        partial.reshape(parts, piece, rows_tile), ("y", "zh"), 0, 0, tiled=True
    )
    own_quarter = own_quarter * jnp.bfloat16(0.5)
    own_columns = lax.all_gather(own_quarter, "y", axis=0, tiled=True)
    total = jnp.sum(shares.astype(jnp.float32), axis=0)
    projected = total.astype(jnp.bfloat16)
    halved = projected * jnp.bfloat16(0.5)

    crossed = lax.ppermute(projected, NAMES, crossing_of_sums())
    pair = lax.all_gather(halved, "zh", axis=0, tiled=True)
    crossed, pair = lax.optimization_barrier((crossed, pair))
    pair, own_columns = lax.optimization_barrier((pair, own_columns))
    row_panel = lax.all_gather(pair, "y", axis=0, tiled=True)
    panel = sent_to_all(crossed, ("x", "zl"), parts).reshape(sample_count, rows_tile)
    other_panel = lax.ppermute(panel, "core", [(0, 1), (1, 0)])

    row_start = ((x * 2 + zl) * 2 + h) * rows_tile
    col_start = (zh * 4 + y) * cols_tile
    whole = jnp.stack([h, row_start, col_start]).astype(jnp.int32)
    scalars = jnp.stack([step_size[0], step_size[0] * threshold[0]])
    return updated_tile(
        whole, scalars, row_panel, own_columns, samples, panel, other_panel, precision
    )


def solution(mesh):
    split = Mesh(mesh.devices.reshape(SIZES), NAMES)
    placed = (P(ROW, COL), P(None, COL), P(), P())
    return jax.shard_map(
        per_device, mesh=split, in_specs=placed, out_specs=P(ROW, COL), check_vma=False
    )
```

```python
import functools
import itertools

import jax
import jax.numpy as jnp
from jax import lax
from jax.experimental import pallas as pl
from jax.experimental.pallas import tpu as pltpu
from jax.sharding import Mesh
from jax.sharding import PartitionSpec as P


SIZES = (4, 2, 2, 2, 4)
NAMES = ("x", "zl", "core", "zh", "y")
ROW = ("x", "zl", "core")
COL = ("zh", "y")


def number(x, zl, h, zh, y):
    return (((x * 2 + zl) * 2 + h) * 2 + zh) * 4 + y


def places():
    return itertools.product(*(range(n) for n in SIZES))


def crossing_of_sums():
    return [
        (number(x, zl, h, zh, y), number(y, zh, h, x // 2, x % 2 * 2 + zl))
        for x, zl, h, zh, y in places()
    ]


def crossing_of_samples():
    return [
        (number(x, zl, h, zh, y), number(zh * 2 + y // 2, y % 2, h, zl ^ zh, (x + y) % 4))
        for x, zl, h, zh, y in places()
    ]


def sent_to_all(array, axes, length):
    copies = jnp.broadcast_to(array[None], (length, *array.shape))
    return lax.all_to_all(copies, axes, 0, 0, tiled=True)


TILE = 256
STRIP = 512


def partial_kernel(samples, precision, out):
    out[...] = lax.dot_general(
        samples[...],
        precision[...].astype(jnp.bfloat16),
        (((1,), (1,)), ((), ())),
        preferred_element_type=jnp.float32,
    ).astype(jnp.bfloat16)


def partial_sums(samples, precision):
    count, width = samples.shape
    rows = precision.shape[0]
    return pl.pallas_call(
        partial_kernel,
        out_shape=jax.ShapeDtypeStruct((count, rows), jnp.bfloat16),
        grid=(rows // STRIP,),
        in_specs=[
            pl.BlockSpec((count, width), lambda r: (0, 0)),
            pl.BlockSpec((STRIP, width), lambda r: (r, 0)),
        ],
        out_specs=pl.BlockSpec((count, STRIP), lambda r: (0, r)),
        compiler_params=pltpu.CompilerParams(vmem_limit_bytes=40 << 20),
        cost_estimate=pl.CostEstimate(
            flops=2 * count * rows * width, bytes_accessed=14 << 20, transcendentals=0
        ),
        name="partial",
    )(samples, precision)


def update_kernel(
    samples_count, whole, scalars, yr, x0, x1, x2, x3, xc, mine, other, precision, out, kept
):
    deep = x0.shape[0]
    t = pl.program_id(0)
    per_side = pl.num_programs(0) // 2
    contract = (((0,), (0,)), ((), ()))
    step, level = scalars[0], scalars[1]

    def finish(panel):
        total = lax.dot_general(yr[...], xc[...], contract, preferred_element_type=jnp.float32)
        for d, quarter in enumerate((x0, x1, x2, x3)):
            start = pl.multiple_of(whole[3 + d] * deep, deep)
            total = total + lax.dot_general(
                quarter[...],
                panel[pl.ds(start, deep), :],
                contract,
                preferred_element_type=jnp.float32,
            )
        gradient = total * (1.0 / samples_count)
        stepped = precision[...] - step * gradient
        out[...] = stepped - jnp.clip(stepped, -level, level)
        side = (whole[0] + t // per_side) % 2
        offset = whole[2] + (side * per_side + t % per_side) * TILE - whole[1]

        @pl.when((offset >= 0) & (offset < out.shape[0]))
        def _():
            kept[...] = stepped
            rows = pl.ds(pl.multiple_of(offset, TILE), TILE)
            own, shrunk = precision[rows, :], out[rows, :]
            on_diagonal = lax.broadcasted_iota(jnp.int32, own.shape, 0) == (
                lax.broadcasted_iota(jnp.int32, own.shape, 1)
            )
            raised = kept[rows, :] + step / jnp.where(on_diagonal, own, 1.0)
            out[rows, :] = jnp.where(on_diagonal, raised, shrunk)

    @pl.when(t < per_side)
    def _():
        finish(mine)

    @pl.when(t >= per_side)
    def _():
        finish(other)


def updated_tile(whole, scalars, yr, quarters, xc, mine, other, precision):
    rows, cols = precision.shape
    count = xc.shape[0]
    per_side = cols // TILE // 2
    inside = pl.BlockSpec(memory_space=pltpu.VMEM)

    def column(t, whole):
        return 0, (whole[0] + t // per_side) % 2 * per_side + t % per_side

    tile = pl.BlockSpec((rows, TILE), column)
    yr = pltpu.with_memory_space_constraint(yr, pltpu.HBM)
    return pl.pallas_call(
        functools.partial(update_kernel, count),
        out_shape=jax.ShapeDtypeStruct(precision.shape, precision.dtype),
        grid_spec=pltpu.PrefetchScalarGridSpec(
            num_scalar_prefetch=1,
            grid=(2 * per_side,),
            in_specs=[
                pl.BlockSpec(memory_space=pltpu.SMEM),
                pl.BlockSpec(yr.shape, lambda t, whole: (0, 0)),
                inside,
                inside,
                inside,
                inside,
                pl.BlockSpec((count, TILE), column),
                pl.BlockSpec((count, TILE), lambda t, whole: (0, jnp.minimum(t, per_side - 1))),
                pl.BlockSpec((count, TILE), lambda t, whole: (0, jnp.maximum(t - per_side, 0))),
                tile,
            ],
            out_specs=tile,
            scratch_shapes=[pltpu.VMEM((rows, TILE), jnp.float32)],
        ),
        compiler_params=pltpu.CompilerParams(vmem_limit_bytes=48 << 20),
        cost_estimate=pl.CostEstimate(
            flops=4 * rows * cols * count, bytes_accessed=28 << 20, transcendentals=0
        ),
        name="update",
    )(whole, scalars, yr, *quarters, xc, mine, other, precision)


def per_device(precision, samples, step_size, threshold):
    rows_tile, cols_tile = precision.shape
    sample_count = samples.shape[0]
    x, zl, h, zh, y = (lax.axis_index(a) for a in NAMES)
    parts = 8
    piece = sample_count // parts

    mine = lax.dynamic_slice(
        samples, ((x + y) % 4 * 2 * piece, h * rows_tile), (2 * piece, rows_tile)
    )
    own_quarter = lax.ppermute(mine, NAMES, crossing_of_samples())
    partial = partial_sums(samples, precision)
    shares = lax.all_to_all(partial.reshape(parts, piece, rows_tile), ("y", "zh"), 0, 0, tiled=True)
    own_quarter = own_quarter * jnp.bfloat16(0.5)
    total = jnp.sum(shares.astype(jnp.float32), axis=0)
    projected = total.astype(jnp.bfloat16)
    halved = projected * jnp.bfloat16(0.5)

    crossed = lax.ppermute(projected, NAMES, crossing_of_sums())
    pair = lax.all_gather(halved, "zh", axis=0, tiled=True)
    crossed, pair = lax.optimization_barrier((crossed, pair))
    own_quarter, pair = lax.optimization_barrier((own_quarter, pair))
    row_panel = lax.all_gather(pair, "y", axis=0, tiled=True)
    quarters = [own_quarter]
    for turn in (1, 3, 2):
        moves = [(i, (i + turn) % 4) for i in range(4)]
        quarters.append(lax.ppermute(own_quarter, "y", moves))
    panel = sent_to_all(crossed, ("x", "zl"), parts).reshape(sample_count, rows_tile)
    other_panel = lax.ppermute(panel, "core", [(0, 1), (1, 0)])

    row_start = ((x * 2 + zl) * 2 + h) * rows_tile
    col_start = (zh * 4 + y) * cols_tile
    places_of = [(y - turn) % 4 for turn in (0, 1, 3, 2)]
    whole = jnp.stack([h, row_start, col_start, *places_of]).astype(jnp.int32)
    scalars = jnp.stack([step_size[0], step_size[0] * threshold[0]])
    return updated_tile(
        whole, scalars, row_panel, quarters, samples, panel, other_panel, precision
    )


def solution(mesh):
    split = Mesh(mesh.devices.reshape(SIZES), NAMES)
    placed = (P(ROW, COL), P(None, COL), P(), P())
    return jax.shard_map(
        per_device, mesh=split, in_specs=placed, out_specs=P(ROW, COL), check_vma=False
    )
```

```python
import itertools

import jax
import jax.numpy as jnp
from jax import lax
from jax.experimental import pallas as pl
from jax.experimental.pallas import tpu as pltpu
from jax.sharding import Mesh
from jax.sharding import PartitionSpec as P


SIZES = (4, 2, 2, 2, 4)
NAMES = ("x", "zl", "core", "zh", "y")
ROW = ("x", "zl", "core")
COL = ("zh", "y")


def number(x, zl, h, zh, y):
    return (((x * 2 + zl) * 2 + h) * 2 + zh) * 4 + y


def places():
    return itertools.product(*(range(n) for n in SIZES))


def crossing_of_sums():
    return [
        (number(x, zl, h, zh, y), number((x + y) % 4, zh, h, x // 2, x % 2 * 2 + zl))
        for x, zl, h, zh, y in places()
    ]


def crossing_of_samples():
    return [
        (number(x, zl, h, zh, y), number(zh * 2 + y // 2, y % 2, h, zl ^ zh, (x + y) % 4))
        for x, zl, h, zh, y in places()
    ]


def sent_to_all(array, axes, length):
    copies = jnp.broadcast_to(array[None], (length, *array.shape))
    return lax.all_to_all(copies, axes, 0, 0, tiled=True)


TILE = 256
STRIP = 256


def partial_kernel(samples, precision, out):
    out[...] = lax.dot_general(
        samples[...],
        precision[...].astype(jnp.bfloat16),
        (((1,), (1,)), ((), ())),
        preferred_element_type=jnp.float32,
    ).astype(jnp.bfloat16)


def partial_sums(samples, precision):
    count, width = samples.shape
    rows = precision.shape[0]
    samples = pltpu.with_memory_space_constraint(samples, pltpu.HBM)
    precision = pltpu.with_memory_space_constraint(precision, pltpu.HBM)
    return pl.pallas_call(
        partial_kernel,
        out_shape=jax.ShapeDtypeStruct((count, rows), jnp.bfloat16),
        grid=(rows // STRIP,),
        in_specs=[
            pl.BlockSpec((count, width), lambda r: (0, 0)),
            pl.BlockSpec((STRIP, width), lambda r: (r, 0)),
        ],
        out_specs=pl.BlockSpec((count, STRIP), lambda r: (0, r)),
        compiler_params=pltpu.CompilerParams(vmem_limit_bytes=40 << 20),
        cost_estimate=pl.CostEstimate(
            flops=2 * count * rows * width, bytes_accessed=14 << 20, transcendentals=0
        ),
        name="partial",
    )(samples, precision)


def update_kernel(
    whole, scales, steps, yr, x0, x1, x2, x3, xc, mine, other, precision, out, kept
):
    deep = x0.shape[0]
    t = pl.program_id(0)
    per_side = pl.num_programs(0) // 2
    contract = (((0,), (0,)), ((), ()))
    scale, step, level = scales[0], scales[1], steps[1]

    def finish(panel):
        total = lax.dot_general(yr[...], xc[...], contract, preferred_element_type=jnp.float32)
        for d, quarter in enumerate((x0, x1, x2, x3)):
            start = pl.multiple_of(whole[3 + d] * deep, deep)
            total = total + lax.dot_general(
                quarter[...],
                panel[pl.ds(start, deep), :],
                contract,
                preferred_element_type=jnp.float32,
            )
        stepped = precision[...] - scale * total
        out[...] = stepped - jnp.clip(stepped, -level, level)
        side = (whole[0] + t // per_side) % 2
        offset = whole[2] + (side * per_side + t % per_side) * TILE - whole[1]

        @pl.when((offset >= 0) & (offset < out.shape[0]))
        def _():
            kept[...] = stepped
            rows = pl.ds(pl.multiple_of(offset, TILE), TILE)
            own, shrunk = precision[rows, :], out[rows, :]
            on_diagonal = lax.broadcasted_iota(jnp.int32, own.shape, 0) == (
                lax.broadcasted_iota(jnp.int32, own.shape, 1)
            )
            raised = kept[rows, :] + step / jnp.where(on_diagonal, own, 1.0)
            out[rows, :] = jnp.where(on_diagonal, raised, shrunk)

    @pl.when(t < per_side)
    def _():
        finish(mine)

    @pl.when(t >= per_side)
    def _():
        finish(other)


def updated_tile(whole, scales, steps, yr, quarters, xc, mine, other, precision):
    rows, cols = precision.shape
    count = xc.shape[0]
    per_side = cols // TILE // 2
    inside = pl.BlockSpec(memory_space=pltpu.VMEM)

    def column(t, whole):
        return 0, (whole[0] + t // per_side) % 2 * per_side + t % per_side

    tile = pl.BlockSpec((rows, TILE), column)
    yr = pltpu.with_memory_space_constraint(yr, pltpu.HBM)
    return pl.pallas_call(
        update_kernel,
        out_shape=jax.ShapeDtypeStruct(precision.shape, precision.dtype),
        grid_spec=pltpu.PrefetchScalarGridSpec(
            num_scalar_prefetch=1,
            grid=(2 * per_side,),
            in_specs=[
                pl.BlockSpec(memory_space=pltpu.SMEM),
                pl.BlockSpec(memory_space=pltpu.SMEM),
                pl.BlockSpec(yr.shape, lambda t, whole: (0, 0)),
                inside,
                inside,
                inside,
                inside,
                pl.BlockSpec((count, TILE), column),
                pl.BlockSpec((count, TILE), lambda t, whole: (0, jnp.minimum(t, per_side - 1))),
                pl.BlockSpec((count, TILE), lambda t, whole: (0, jnp.maximum(t - per_side, 0))),
                tile,
            ],
            out_specs=tile,
            scratch_shapes=[pltpu.VMEM((rows, TILE), jnp.float32)],
        ),
        compiler_params=pltpu.CompilerParams(vmem_limit_bytes=48 << 20),
        cost_estimate=pl.CostEstimate(
            flops=4 * rows * cols * count, bytes_accessed=28 << 20, transcendentals=0
        ),
        name="update",
    )(whole, scales, steps, yr, *quarters, xc, mine, other, precision)


def joined(own, other, place):
    upper = jnp.where(place == 0, own, other)
    lower = jnp.where(place == 0, other, own)
    return jnp.concatenate([upper, lower], axis=0)


def per_device(precision, samples, step_size, threshold):
    rows_tile, cols_tile = precision.shape
    sample_count = samples.shape[0]
    x, zl, h, zh, y = (lax.axis_index(a) for a in NAMES)
    parts = 8
    piece = sample_count // parts

    block = (x + y) % 4 * 2 + (zl ^ zh)
    mine = lax.dynamic_slice(samples, (block * piece, h * rows_tile), (piece, rows_tile))
    own_eighth = lax.ppermute(mine, NAMES, crossing_of_samples())
    partial = partial_sums(samples, precision)
    shares = lax.all_to_all(partial.reshape(parts, piece, rows_tile), ("y", "zh"), 0, 0, tiled=True)
    own_eighth = own_eighth * jnp.bfloat16(0.5)
    other_eighth = lax.ppermute(own_eighth, "zh", [(0, 1), (1, 0)])
    steps = jnp.stack([step_size[0], step_size[0] * threshold[0]])
    total = jnp.sum(shares.astype(jnp.float32), axis=0)
    projected = total.astype(jnp.bfloat16)
    halved = projected * jnp.bfloat16(0.5)

    crossed = lax.ppermute(projected, NAMES, crossing_of_sums())
    other = lax.ppermute(halved, "zh", [(0, 1), (1, 0)])
    pair = joined(halved, other, zh)
    later, _, pair = lax.optimization_barrier((step_size, threshold, pair))
    row_panel = lax.all_gather(pair, "y", axis=0, tiled=True)
    own_quarter = joined(own_eighth, other_eighth, zh)
    quarters = [own_quarter]
    scales = jnp.stack([later[0] * (1.0 / sample_count), later[0]])
    for turn in (1, 3, 2):
        moves = [(i, (i + turn) % 4) for i in range(4)]
        quarters.append(lax.ppermute(own_quarter, "y", moves))
    panel = sent_to_all(crossed, ("x", "zl"), parts).reshape(sample_count, rows_tile)
    other_panel = lax.ppermute(panel, "core", [(0, 1), (1, 0)])

    row_start = ((x * 2 + zl) * 2 + h) * rows_tile
    col_start = (zh * 4 + y) * cols_tile
    places_of = [(y - turn + zh * 2 + y // 2) % 4 for turn in (0, 1, 3, 2)]
    whole = jnp.stack([h, row_start, col_start, *places_of]).astype(jnp.int32)
    return updated_tile(
        whole, scales, steps, row_panel, quarters, samples, panel, other_panel, precision
    )


def solution(mesh):
    split = Mesh(mesh.devices.reshape(SIZES), NAMES)
    placed = (P(ROW, COL), P(None, COL), P(), P())
    return jax.shard_map(
        per_device, mesh=split, in_specs=placed, out_specs=P(ROW, COL), check_vma=False
    )
```

```python
import itertools

import jax
import jax.numpy as jnp
from jax import lax
from jax.experimental import pallas as pl
from jax.experimental.pallas import tpu as pltpu
from jax.sharding import Mesh
from jax.sharding import PartitionSpec as P


SIZES = (4, 2, 2, 2, 4)
NAMES = ("x", "zl", "core", "zh", "y")
ROW = ("x", "zl", "core")
COL = ("zh", "y")


def number(x, zl, h, zh, y):
    return (((x * 2 + zl) * 2 + h) * 2 + zh) * 4 + y


def places():
    return itertools.product(*(range(n) for n in SIZES))


def crossing_of_sums():
    return [
        (number(x, zl, h, zh, y), number((x + y) % 4, zh, h, x // 2, x % 2 * 2 + zl))
        for x, zl, h, zh, y in places()
    ]


def crossing_of_samples():
    return [
        (number(x, zl, h, zh, y), number(zh * 2 + y // 2, y % 2, h, zl ^ zh, (x + y) % 4))
        for x, zl, h, zh, y in places()
    ]


def sent_to_all(array, axes, length):
    copies = jnp.broadcast_to(array[None], (length, *array.shape))
    return lax.all_to_all(copies, axes, 0, 0, tiled=True)


TILE = 256
STRIP = 256


def partial_kernel(samples, precision, out):
    out[...] = lax.dot_general(
        samples[...],
        precision[...].astype(jnp.bfloat16),
        (((1,), (1,)), ((), ())),
        preferred_element_type=jnp.float32,
    ).astype(jnp.bfloat16)


def partial_sums(samples, precision):
    count, width = samples.shape
    rows = precision.shape[0]
    samples = pltpu.with_memory_space_constraint(samples, pltpu.HBM)
    precision = pltpu.with_memory_space_constraint(precision, pltpu.HBM)
    return pl.pallas_call(
        partial_kernel,
        out_shape=jax.ShapeDtypeStruct((count, rows), jnp.bfloat16),
        grid=(rows // STRIP,),
        in_specs=[
            pl.BlockSpec((count, width), lambda r: (0, 0)),
            pl.BlockSpec((STRIP, width), lambda r: (r, 0)),
        ],
        out_specs=pl.BlockSpec((count, STRIP), lambda r: (0, r)),
        compiler_params=pltpu.CompilerParams(vmem_limit_bytes=40 << 20),
        cost_estimate=pl.CostEstimate(
            flops=2 * count * rows * width, bytes_accessed=14 << 20, transcendentals=0
        ),
        name="partial",
    )(samples, precision)


def update_kernel(
    whole, scales, steps, y0, y1, y2, y3, x0, x1, x2, x3, xc, mine, other, precision, out, kept
):
    deep = x0.shape[0]
    t = pl.program_id(0)
    per_side = pl.num_programs(0) // 2
    scale, step, level = scales[0], scales[1], steps[1]

    def product(quarters, panel, first_place):
        total = None
        for d, quarter in enumerate(quarters):
            start = pl.multiple_of(whole[first_place + d] * deep, deep)
            term = lax.dot_general(
                quarter[...],
                panel[pl.ds(start, deep), :],
                (((0,), (0,)), ((), ())),
                preferred_element_type=jnp.float32,
            )
            total = term if total is None else total + term
        return total

    def finish(panel):
        total = product((x0, x1, x2, x3), panel, 7) + product((y0, y1, y2, y3), xc, 3)
        stepped = precision[...] - scale * total
        out[...] = stepped - jnp.clip(stepped, -level, level)
        side = (whole[0] + t // per_side) % 2
        offset = whole[2] + (side * per_side + t % per_side) * TILE - whole[1]

        @pl.when((offset >= 0) & (offset < out.shape[0]))
        def _():
            kept[...] = stepped
            rows = pl.ds(pl.multiple_of(offset, TILE), TILE)
            own, shrunk = precision[rows, :], out[rows, :]
            on_diagonal = lax.broadcasted_iota(jnp.int32, own.shape, 0) == (
                lax.broadcasted_iota(jnp.int32, own.shape, 1)
            )
            raised = kept[rows, :] + step / jnp.where(on_diagonal, own, 1.0)
            out[rows, :] = jnp.where(on_diagonal, raised, shrunk)

    @pl.when(t < per_side)
    def _():
        finish(mine)

    @pl.when(t >= per_side)
    def _():
        finish(other)


def updated_tile(whole, scales, steps, row_quarters, quarters, xc, mine, other, precision):
    rows, cols = precision.shape
    count = xc.shape[0]
    per_side = cols // TILE // 2
    inside = pl.BlockSpec(memory_space=pltpu.VMEM)

    def column(t, whole):
        return 0, (whole[0] + t // per_side) % 2 * per_side + t % per_side

    tile = pl.BlockSpec((rows, TILE), column)
    return pl.pallas_call(
        update_kernel,
        out_shape=jax.ShapeDtypeStruct(precision.shape, precision.dtype),
        grid_spec=pltpu.PrefetchScalarGridSpec(
            num_scalar_prefetch=1,
            grid=(2 * per_side,),
            in_specs=[
                pl.BlockSpec(memory_space=pltpu.SMEM),
                pl.BlockSpec(memory_space=pltpu.SMEM),
                *[inside] * 8,
                pl.BlockSpec((count, TILE), column),
                pl.BlockSpec((count, TILE), lambda t, whole: (0, jnp.minimum(t, per_side - 1))),
                pl.BlockSpec((count, TILE), lambda t, whole: (0, jnp.maximum(t - per_side, 0))),
                tile,
            ],
            out_specs=tile,
            scratch_shapes=[pltpu.VMEM((rows, TILE), jnp.float32)],
        ),
        compiler_params=pltpu.CompilerParams(vmem_limit_bytes=48 << 20),
        cost_estimate=pl.CostEstimate(
            flops=4 * rows * cols * count, bytes_accessed=28 << 20, transcendentals=0
        ),
        name="update",
    )(whole, scales, steps, *row_quarters, *quarters, xc, mine, other, precision)


TURNS = (0, 1, 3, 2)


def spread_along_y(quarter):
    return [quarter] + [
        lax.ppermute(quarter, "y", [(i, (i + turn) % 4) for i in range(4)]) for turn in TURNS[1:]
    ]


def joined(own, other, place):
    upper = jnp.where(place == 0, own, other)
    lower = jnp.where(place == 0, other, own)
    return jnp.concatenate([upper, lower], axis=0)


def per_device(precision, samples, step_size, threshold):
    rows_tile, cols_tile = precision.shape
    sample_count = samples.shape[0]
    x, zl, h, zh, y = (lax.axis_index(a) for a in NAMES)
    parts = 8
    piece = sample_count // parts

    block = (x + y) % 4 * 2 + (zl ^ zh)
    mine = lax.dynamic_slice(samples, (block * piece, h * rows_tile), (piece, rows_tile))
    own_eighth = lax.ppermute(mine, NAMES, crossing_of_samples())
    partial = partial_sums(samples, precision)
    shares = lax.all_to_all(partial.reshape(parts, piece, rows_tile), ("y", "zh"), 0, 0, tiled=True)
    own_eighth = own_eighth * jnp.bfloat16(0.5)
    other_eighth = lax.ppermute(own_eighth, "zh", [(0, 1), (1, 0)])
    steps = jnp.stack([step_size[0], step_size[0] * threshold[0]])
    total = jnp.sum(shares.astype(jnp.float32), axis=0)
    projected = total.astype(jnp.bfloat16)
    halved = projected * jnp.bfloat16(0.5)

    crossed = lax.ppermute(projected, NAMES, crossing_of_sums())
    other = lax.ppermute(halved, "zh", [(0, 1), (1, 0)])
    pair = joined(halved, other, zh)
    later, _, pair = lax.optimization_barrier((step_size, threshold, pair))
    row_quarters = spread_along_y(pair)
    own_quarter = joined(own_eighth, other_eighth, zh)
    quarters = spread_along_y(own_quarter)
    scales = jnp.stack([later[0] * (1.0 / sample_count), later[0]])
    panel = sent_to_all(crossed, ("x", "zl"), parts).reshape(sample_count, rows_tile)
    other_panel = lax.ppermute(panel, "core", [(0, 1), (1, 0)])

    row_start = ((x * 2 + zl) * 2 + h) * rows_tile
    col_start = (zh * 4 + y) * cols_tile
    places_of = [(y - turn) % 4 for turn in TURNS]
    places_of += [(place + zh * 2 + y // 2) % 4 for place in places_of]
    whole = jnp.stack([h, row_start, col_start, *places_of]).astype(jnp.int32)
    return updated_tile(
        whole, scales, steps, row_quarters, quarters, samples, panel, other_panel, precision
    )


def solution(mesh):
    split = Mesh(mesh.devices.reshape(SIZES), NAMES)
    placed = (P(ROW, COL), P(None, COL), P(), P())
    return jax.shard_map(
        per_device, mesh=split, in_specs=placed, out_specs=P(ROW, COL), check_vma=False
    )
```

```python
import itertools

import jax
import jax.numpy as jnp
from jax import lax
from jax.experimental import pallas as pl
from jax.experimental.pallas import tpu as pltpu
from jax.sharding import Mesh
from jax.sharding import PartitionSpec as P


SIZES = (4, 2, 2, 2, 4)
NAMES = ("x", "zl", "core", "zh", "y")
ROW = ("x", "zl", "core")
COL = ("zh", "y")


def number(x, zl, h, zh, y):
    return (((x * 2 + zl) * 2 + h) * 2 + zh) * 4 + y


def places():
    return itertools.product(*(range(n) for n in SIZES))


def crossing_of_sums():
    return [
        (number(x, zl, h, zh, y), number((x + y) % 4, zh, h, x // 2, x % 2 * 2 + zl))
        for x, zl, h, zh, y in places()
    ]


def crossing_of_samples():
    return [
        (number(x, zl, h, zh, y), number(zh * 2 + y // 2, y % 2, h, zl ^ zh, (x + y) % 4))
        for x, zl, h, zh, y in places()
    ]


def sent_to_all(array, axes, length):
    copies = jnp.broadcast_to(array[None], (length, *array.shape))
    return lax.all_to_all(copies, axes, 0, 0, tiled=True)


TILE = 256
STRIP = 256


def partial_kernel(samples, precision, out):
    out[...] = lax.dot_general(
        samples[...],
        precision[...].astype(jnp.bfloat16),
        (((1,), (1,)), ((), ())),
        preferred_element_type=jnp.float32,
    ).astype(jnp.bfloat16)


def partial_sums(samples, precision):
    count, width = samples.shape
    rows = precision.shape[0]
    samples = pltpu.with_memory_space_constraint(samples, pltpu.HBM)
    precision = pltpu.with_memory_space_constraint(precision, pltpu.HBM)
    return pl.pallas_call(
        partial_kernel,
        out_shape=jax.ShapeDtypeStruct((count, rows), jnp.bfloat16),
        grid=(rows // STRIP,),
        in_specs=[
            pl.BlockSpec((count, width), lambda r: (0, 0)),
            pl.BlockSpec((STRIP, width), lambda r: (r, 0)),
        ],
        out_specs=pl.BlockSpec((count, STRIP), lambda r: (0, r)),
        compiler_params=pltpu.CompilerParams(vmem_limit_bytes=40 << 20),
        cost_estimate=pl.CostEstimate(
            flops=2 * count * rows * width, bytes_accessed=14 << 20, transcendentals=0
        ),
        name="partial",
    )(samples, precision)


CONTRACT = (((0,), (0,)), ((), ()))


def in_hbm(*arrays):
    return [pltpu.with_memory_space_constraint(a, pltpu.HBM) for a in arrays]


def sum_of_products(whole, first_place, quarters, panel):
    total = None
    for d, quarter in enumerate(quarters):
        deep = quarter.shape[0]
        start = pl.multiple_of(whole[first_place + d] * deep, deep)
        term = lax.dot_general(
            quarter, panel[pl.ds(start, deep), :], CONTRACT, preferred_element_type=jnp.float32
        )
        total = term if total is None else total + term
    return total


def update_kernel(
    whole, scales, steps, y0, y1, y2, y3, y4, x0, x1, x2, x3, x4, xc, panel, precision, *rest
):
    out, kept = rest[-2:]
    t = pl.program_id(0)
    scale, step, level = scales[0], scales[1], steps[1]
    opposite = jnp.concatenate([y3[...], y4[...]], axis=0)
    total = sum_of_products(whole, 3, (y0[...], y1[...], y2[...], opposite), xc)
    turned = jnp.concatenate([x3[...], x4[...]], axis=0)
    total = total + sum_of_products(whole, 7, (x0[...], x1[...], x2[...], turned), panel)
    stepped = precision[...] - scale * total
    out[...] = stepped - jnp.clip(stepped, -level, level)
    offset = whole[2] + (whole[0] * pl.num_programs(0) + t) * TILE - whole[1]

    @pl.when((offset >= 0) & (offset < out.shape[0]))
    def _():
        kept[...] = stepped
        rows = pl.ds(pl.multiple_of(offset, TILE), TILE)
        own, shrunk = precision[rows, :], out[rows, :]
        on_diagonal = lax.broadcasted_iota(jnp.int32, own.shape, 0) == (
            lax.broadcasted_iota(jnp.int32, own.shape, 1)
        )
        raised = kept[rows, :] + step / jnp.where(on_diagonal, own, 1.0)
        out[rows, :] = jnp.where(on_diagonal, raised, shrunk)


def updated_half(whole, scales, steps, row_quarters, quarters, xc, panel, precision, into):
    rows, _ = precision.shape
    count, width = panel.shape
    per_side = width // TILE
    inside = pl.BlockSpec(memory_space=pltpu.VMEM)
    scalar = pl.BlockSpec(memory_space=pltpu.SMEM)
    tile = pl.BlockSpec((rows, TILE), lambda t, whole: (0, whole[0] * per_side + t))
    xc, precision = in_hbm(xc, precision)
    arrays = [whole, scales, steps, *row_quarters, *quarters, xc, panel, precision]
    specs = [scalar] * 2 + [inside] * 10
    specs += [
        pl.BlockSpec((count, TILE), lambda t, whole: (0, whole[0] * per_side + t)),
        pl.BlockSpec((count, TILE), lambda t, whole: (0, t)),
        tile,
    ]
    aliases = {}
    if into is not None:
        aliases = {len(arrays): 0}
        arrays.append(into)
        specs.append(pl.BlockSpec(memory_space=pl.ANY))
    return pl.pallas_call(
        update_kernel,
        out_shape=jax.ShapeDtypeStruct(precision.shape, precision.dtype),
        grid_spec=pltpu.PrefetchScalarGridSpec(
            num_scalar_prefetch=1,
            grid=(per_side,),
            in_specs=specs,
            out_specs=tile,
            scratch_shapes=[pltpu.VMEM((rows, TILE), jnp.float32)],
        ),
        input_output_aliases=aliases,
        compiler_params=pltpu.CompilerParams(vmem_limit_bytes=48 << 20),
        cost_estimate=pl.CostEstimate(
            flops=4 * rows * width * count, bytes_accessed=14 << 20, transcendentals=0
        ),
        name="update",
    )(*arrays)


TURNS = (0, 1, 3, 2)


def moved_along_y(array, turn):
    return lax.ppermute(array, "y", [(i, (i + turn) % 4) for i in range(4)])


def onward_along_y(before, after):
    half = before.shape[0] // 2
    return [moved_along_y(before[:half], 1), moved_along_y(after[half:], 3)]


def joined(own, other, place):
    upper = jnp.where(place == 0, own, other)
    lower = jnp.where(place == 0, other, own)
    return jnp.concatenate([upper, lower], axis=0)


def per_device(precision, samples, step_size, threshold):
    rows_tile, cols_tile = precision.shape
    sample_count = samples.shape[0]
    x, zl, h, zh, y = (lax.axis_index(a) for a in NAMES)
    parts = 8
    piece = sample_count // parts

    block = (x + y) % 4 * 2 + (zl ^ zh)
    mine = lax.dynamic_slice(samples, (block * piece, h * rows_tile), (piece, rows_tile))
    own_eighth = lax.ppermute(mine, NAMES, crossing_of_samples())
    partial = partial_sums(samples, precision)
    shares = lax.all_to_all(partial.reshape(parts, piece, rows_tile), ("y", "zh"), 0, 0, tiled=True)
    own_eighth = own_eighth * jnp.bfloat16(0.5)
    other_eighth = lax.ppermute(own_eighth, "zh", [(0, 1), (1, 0)])
    steps = jnp.stack([step_size[0], step_size[0] * threshold[0]])
    total = jnp.sum(shares.astype(jnp.float32), axis=0)
    projected = total.astype(jnp.bfloat16)
    halved = projected * jnp.bfloat16(0.5)

    crossed = lax.ppermute(projected, NAMES, crossing_of_sums())
    other = lax.ppermute(halved, "zh", [(0, 1), (1, 0)])
    pair = joined(halved, other, zh)
    later, _, pair = lax.optimization_barrier((step_size, threshold, pair))
    row_quarters = [pair, moved_along_y(pair, 1), moved_along_y(pair, 3)]
    own_quarter = joined(own_eighth, other_eighth, zh)
    quarters = [own_quarter, moved_along_y(own_quarter, 1), moved_along_y(own_quarter, 3)]
    quarters += onward_along_y(*quarters[1:])
    row_quarters += onward_along_y(*row_quarters[1:])
    scales = jnp.stack([later[0] * (1.0 / sample_count), later[0]])
    row_start = ((x * 2 + zl) * 2 + h) * rows_tile
    col_start = (zh * 4 + y) * cols_tile
    places_of = [(y - turn) % 4 for turn in TURNS]
    places_of += [(place + zh * 2 + y // 2) % 4 for place in places_of]
    fixed = [row_start, col_start, *places_of]
    own_side = jnp.stack([h, *fixed]).astype(jnp.int32)
    other_side = jnp.stack([1 - h, *fixed]).astype(jnp.int32)
    panel = sent_to_all(crossed, ("x", "zl"), parts).reshape(sample_count, rows_tile)
    other_panel = lax.ppermute(panel, "core", [(0, 1), (1, 0)])
    operands = (scales, steps, row_quarters, quarters, samples)
    half_done = updated_half(own_side, *operands, panel, precision, None)
    return updated_half(other_side, *operands, other_panel, precision, half_done)


def solution(mesh):
    split = Mesh(mesh.devices.reshape(SIZES), NAMES)
    placed = (P(ROW, COL), P(None, COL), P(), P())
    return jax.shard_map(
        per_device, mesh=split, in_specs=placed, out_specs=P(ROW, COL), check_vma=False
    )
```
